256 devices in a mesh: gx: 16 (over y, x), gy: 16 (over z, core).
Axes of the slice: x: 4, y: 4, z: 8, core: 2. Of those that a mesh axis runs over, the one named last changes fastest.
Arguments:
- occupancy: int32 [4096, 4096], P('gy', 'gx'), may hold values from 0 to 100
- blur_taps: float32 [17], replicated, may hold values from 0.01 to 0.12
- offsets: int32 [16, 16, 2], replicated, may hold values from -10 to 10, as said below
- step_costs: int32 [16, 16], replicated, may hold values from 1 to 16
- value_start: float32 [16, 4096, 4096], P(None, 'gy', 'gx'), may hold values from 0 to 4
Outputs:
- cost_map: float32 [4096, 4096], P('gy', 'gx')
- value: float32 [16, 4096, 4096], P(None, 'gy', 'gx')
The draws below stay inside these ranges and needn't reach their ends.
Inputs may be any that keep to these rules, and one draw needn't show every extreme that they name: `offsets`: every offset lies within -10 .. 10; some primitive's row offset and some primitive's column offset have magnitude exactly 10.
All inputs are finite; a program needn't handle non-finite values.
Results may differ from the reference program's by a relative error of at most 0.00045.
Values may be sent and summed in bfloat16 or wider, within the bound.
A program may use at most 192 MiB of HBM per device.

```python
import math
import jax
import jax.numpy as jnp
from jax import lax

H = 16
P_SIZE = 16
K = 10
R = 8
NX = 4096
NY = 4096


def draw_offsets(key, part):
    keys = jax.random.split(key, 3)
    base = jax.random.randint(keys[0], (H * P_SIZE, 2), -K, K + 1, dtype=jnp.int32)
    picked = jax.random.randint(keys[1], (2,), 0, H * P_SIZE, dtype=jnp.int32)
    signs = jax.random.randint(keys[2], (2,), 0, 2, dtype=jnp.int32) * 2 - 1
    base = base.at[picked[0], 0].set(signs[0] * K)
    base = base.at[picked[1], 1].set(signs[1] * K)
    return base.reshape(H, P_SIZE, 2)


def touch_ends(result, key, smallest, high):
    shape = result.shape
    index_at = [jax.random.randint(jax.random.fold_in(key, axis), (), 0, shape[axis]) for axis in range(len(shape))]
    result = result.at[tuple(index_at)].set(smallest)
    longest = shape.index(max(shape))
    index_at[longest] = (index_at[longest] + 1) % shape[longest]
    return result.at[tuple(index_at)].set(high)


def block_levels(stream_key, dims, shards, least, top_value):
    def one(axis_at, shards_of):
        steps = jax.random.uniform(jax.random.fold_in(jax.random.fold_in(stream_key, 6), axis_at), (shards_of,), jnp.float32, least / len(shards), top_value / len(shards))
        return jnp.repeat(jnp.exp(steps), dims[axis_at] // shards_of).reshape((-1,) + (1,) * (len(dims) - axis_at - 1))

    gain = one(*shards[0])
    for cut in shards[1:]:
        gain = gain * one(*cut)
    return gain


def setup_inputs(seed: int = 0) -> dict:
    key_of = jax.random.split(jax.random.key(seed), 6)
    return {
        "occupancy": touch_ends(jax.random.randint(key_of[0], (NY, NX), 0, 101), jax.random.fold_in(key_of[0], 1), 0, 100).astype(jnp.int32),
        "blur_taps": jnp.clip(jnp.exp(jax.random.uniform(key_of[1], (2 * R + 1,), jnp.float32, math.log(0.01), math.log(0.12))), 0.01, 0.12),
        "offsets": draw_offsets(jax.random.fold_in(key_of[5], 71), 0),
        "step_costs": touch_ends(jax.random.randint(key_of[3], (H, P_SIZE), 1, 17), jax.random.fold_in(key_of[3], 1), 1, 16).astype(jnp.int32),
        "value_start": jnp.clip(4.0 * jax.random.uniform(key_of[4], (H, NY, NX), jnp.float32) ** block_levels(key_of[4], (H, NY, NX), ((1, 16), (2, 16)), -0.2, 0.2), 0.0, 4.0),
    }


wall_value = 40.0


def blur_grid(occupancy, blur_taps):
    occupied = occupancy.astype(jnp.float32)
    width = occupied.shape[1]
    height = occupied.shape[0]
    padded_cols = jnp.pad(occupied, ((0, 0), (R, R)))
    row_blur = blur_taps[0] * padded_cols[:, 0:width]
    for tap_index in range(1, 2 * R + 1):
        row_blur = row_blur + blur_taps[tap_index] * padded_cols[:, tap_index:tap_index + width]
    padded_rows = jnp.pad(row_blur, ((R, R), (0, 0)))
    summed = blur_taps[0] * padded_rows[0:height]
    for tap_index in range(1, 2 * R + 1):
        summed = summed + blur_taps[tap_index] * padded_rows[tap_index:tap_index + height]
    return 0.04 * summed


def relax(arrival, offsets, step_costs):
    out_rows = arrival.shape[1] - 2 * K
    out_cols = arrival.shape[2] - 2 * K
    results = []
    for heading in range(H):
        lowest = None
        for motion in range(P_SIZE):
            turning = (motion % 5) - 2
            target = (heading + turning) % H
            plane = arrival[target]
            start_row = (K + offsets[heading, motion, 0]).astype(jnp.int32)
            start_col = (K + offsets[heading, motion, 1]).astype(jnp.int32)
            window = lax.dynamic_slice(plane, (start_row, start_col), (out_rows, out_cols))
            candidate = step_costs[heading, motion].astype(jnp.float32) * 0.125 + window
            lowest = candidate if lowest is None else jnp.minimum(lowest, candidate)
        results.append(lowest)
    return jnp.stack(results)


def reference(occupancy, blur_taps, offsets, step_costs, value_start):
    cost_map = blur_grid(occupancy, blur_taps)
    value = value_start
    for sweep_index in range(2):
        arrival = cost_map[None] + value
        arrival = jnp.pad(arrival, ((0, 0), (K, K), (K, K)), constant_values=wall_value)
        value = relax(arrival, offsets, step_costs)
    return cost_map, value
```

```python
import jax, jax.numpy as jnp
from jax import lax
from jax.experimental import pallas as pl
from jax.experimental.pallas import tpu as pltpu
from jax.sharding import PartitionSpec as P

H = 16; P_SIZE = 16; K = 10; R = 8
LS = 9
NL = 32
NQ = 4
XS = 72
SE = LS + 2 * K
XE = 96
WALL = 40.0
OUT_MAP = 1e9
f32 = jnp.float32

def lane(n=8):
    return lax.broadcasted_iota(jnp.int32, (n, 128), 1)

def blur(taps, occ4, ct4, mt4, cost, limits):
    r_lo, r_hi, c_lo, c_hi = limits
    @pl.loop(0, 39)
    def _(i):
        row = pl.multiple_of(i * 8, 8)
        y = row + lax.broadcasted_iota(jnp.int32, (8, 128), 0)
        in_rows = (y >= r_lo) & (y < r_hi)
        for q in range(NQ):
            vb = taps[0] * occ4[q, pl.ds(row, 8), :]
            for t in range(1, 2 * R + 1):
                vb = vb + taps[t] * occ4[q, pl.ds(row + t, 8), :]
            hb = taps[0] * vb
            for t in range(1, 2 * R + 1):
                hb = hb + taps[t] * pltpu.roll(vb, 128 - t, 1)
            c = 0.04 * hb
            x = lane() + q * XS
            inside = in_rows & (x >= c_lo) & (x < c_hi)
            ct4[q, pl.ds(row, 8), :] = c
            mt4[q, pl.ds(row, 8), :] = jnp.where(inside, c, OUT_MAP)
    @pl.loop(0, 32)
    def _(i):
        g = [ct4[q, pl.ds(i * 8 + 20, 8), :] for q in range(NQ)]
        g = [pltpu.roll(v, s, 1) for v, s in zip(g, (108, 52, 124, 68))]
        m = lane()
        row = pl.multiple_of(i * 8, 8)
        cost[pl.ds(row, 8), 0:128] = jnp.where(m < 52, g[0], jnp.where(m < 124, g[1], g[2]))
        cost[pl.ds(row, 8), 128:256] = jnp.where(m < 68, g[2], g[3])

def kernel_b(offs, costs, taps, v4, occ4, cost, value, a1, a2, ct4, mt4, cl, vin, tmp4, o4, ob, vst, isem, osem):
    gx = lax.axis_index("gx"); gy = lax.axis_index("gy")
    r_lo = 20 - 256 * gy; r_hi = 20 + 256 * (lax.axis_size("gy") - gy)
    c_lo = 20 - 256 * gx; c_hi = 20 + 256 * (lax.axis_size("gx") - gx)
    def vload(t, slot):
        return pltpu.make_async_copy(v4.at[t], vin.at[slot], isem.at[slot])
    vload(0, 0).start()
    blur(taps, occ4, ct4, mt4, cost, (r_lo, r_hi, c_lo, c_hi))
    @pl.loop(0, LS)
    def _(s):
        x = jnp.concatenate([mt4[q, pl.ds(s + K, NL, stride=LS), :] for q in range(NQ)], axis=0)
        cl[s] = jnp.transpose(x)[:XE]
    @pl.loop(0, H)
    def _(t):
        slot = lax.rem(t, 2)
        vload(t, slot).wait()
        @pl.when(t + 1 < H)
        def _():
            vload(t + 1, 1 - slot).start()
        @pl.loop(0, 39)
        def _(i):
            row = pl.multiple_of(i * 8, 8)
            for q in range(NQ):
                c = mt4[q, pl.ds(row, 8), :]
                tmp4[q, pl.ds(row, 8), :] = jnp.where(c > 1e8, WALL, vin[slot, q, pl.ds(row, 8), :] + c)
        @pl.loop(0, SE)
        def _(s):
            x = jnp.concatenate([tmp4[q, pl.ds(s, NL, stride=LS), :] for q in range(NQ)], axis=0)
            a1[pl.ds(pl.multiple_of((t * SE + s) * XE, 8), XE), :] = jnp.transpose(x)[:XE]
    def scalars(h):
        out = []
        for p in range(P_SIZE):
            q = h * P_SIZE + p
            t = lax.rem(h + (p % 5) + H - 2, H)
            out.append(((t * SE + offs[2 * q] + K) * XE + offs[2 * q + 1] + K, costs[q].astype(f32) * 0.125))
        return out
    def lowest(a, sc, s):
        acc = None
        for base, c in sc:
            v = a[pl.ds(base + s * XE, XS), :] + c
            acc = v if acc is None else jnp.minimum(acc, v)
        return acc
    @pl.loop(0, H)
    def _(h):
        sc = scalars(h)
        @pl.loop(0, LS)
        def _(s):
            acc = lowest(a1, sc, s)
            c = cl[s, K:K + XS, :]
            arr = jnp.where(c > 1e8, WALL, acc + c)
            r0 = pl.multiple_of((h * SE + s + K) * XE, 8)
            a2[pl.ds(r0 + K, XS), :] = arr
            lo = pltpu.roll(a2[pl.ds(r0 + XS, 8), :], NL, 1)
            lo2 = pltpu.roll(a2[pl.ds(r0 + XS + 2, 8), :], NL, 1)
            hi = pltpu.roll(a2[pl.ds(r0 + K, 8), :], 128 - NL, 1)
            hi2 = pltpu.roll(a2[pl.ds(r0 + K + 2, 8), :], 128 - NL, 1)
            a2[pl.ds(r0, 8), :] = lo
            a2[pl.ds(r0 + 2, 8), :] = lo2
            a2[pl.ds(r0 + XS + K, 8), :] = hi
            a2[pl.ds(r0 + XS + K + 2, 8), :] = hi2
            full = a2[pl.ds(r0, XE), :]
            a2[pl.ds(pl.multiple_of(r0 - LS * XE, 8), XE), :] = pltpu.roll(full, 1, 1)
            a2[pl.ds(pl.multiple_of(r0 + LS * XE, 8), XE), :] = pltpu.roll(full, 127, 1)
            @pl.when(s == LS - 1)
            def _():
                a2[pl.ds(pl.multiple_of(r0 - 2 * LS * XE, 8), XE), :] = pltpu.roll(full, 2, 1)
            @pl.when(s == 0)
            def _():
                a2[pl.ds(pl.multiple_of(r0 + 2 * LS * XE, 8), XE), :] = pltpu.roll(full, 126, 1)
    def vstore(h, slot):
        return pltpu.make_async_copy(vst.at[slot], value.at[h], osem.at[slot])
    @pl.loop(0, H)
    def _(h):
        sc = scalars(h)
        slot = lax.rem(h, 2)
        @pl.loop(0, LS)
        def _(s):
            ob[0:XS, :] = lowest(a2, sc, s)
            x = jnp.transpose(ob[...])
            for q in range(NQ):
                o4[q, pl.ds(s, NL, stride=LS), :] = x[q * NL:(q + 1) * NL]
        @pl.when(h >= 2)
        def _():
            vstore(h, slot).wait()
        @pl.loop(0, 32)
        def _(i):
            g = [o4[q, pl.ds(i * 8 + K, 8), :] for q in range(NQ)]
            g = [pltpu.roll(v, s, 1) for v, s in zip(g, (118, 62, 6, 78))]
            m = lane()
            row = pl.multiple_of(i * 8, 8)
            vst[slot, pl.ds(row, 8), 0:128] = jnp.where(m < 62, g[0], g[1])
            vst[slot, pl.ds(row, 8), 128:256] = jnp.where(m < 6, g[1], jnp.where(m < 78, g[2], g[3]))
        vstore(h, slot).start()
    vstore(0, 0).wait()
    vstore(1, 1).wait()

def call_b(offsets, step_costs, blur_taps, v4, occ4):
    S = pltpu.SMEM; V = pltpu.VMEM
    sp = lambda m: pl.BlockSpec(memory_space=m)
    return pl.pallas_call(
        kernel_b,
        out_shape=(jax.ShapeDtypeStruct((256, 256), f32), jax.ShapeDtypeStruct((H, 256, 256), f32)),
        in_specs=[sp(S), sp(S), sp(S), sp(pl.ANY), sp(V)],
        out_specs=(sp(V), sp(pl.ANY)),
        scratch_shapes=[V((H * SE * XE, 128), f32), V((H * SE * XE, 128), f32),
            V((NQ, 312, 128), f32), V((NQ, 312, 128), f32), V((LS, XE, 128), f32),
            V((2, NQ, 312, 128), f32), V((NQ, 312, 128), f32), V((NQ, NL * LS, 128), f32), V((128, 128), f32),
            V((2, 256, 256), f32), pltpu.SemaphoreType.DMA((2,)), pltpu.SemaphoreType.DMA((2,))],
        compiler_params=pltpu.CompilerParams(vmem_limit_bytes=63 * 2**20),
    )(offsets.reshape(-1), step_costs.reshape(-1), blur_taps, v4, occ4)


def with_halo(block, sides, width):
    for axis, dim in sides:
        count = lax.axis_size(axis)
        forward = [(i, i + 1) for i in range(count - 1)]
        backward = [(target, source) for source, target in forward]
        low = lax.ppermute(lax.slice_in_dim(block, block.shape[dim] - width, None, axis=dim), axis, forward)
        high = lax.ppermute(lax.slice_in_dim(block, 0, width, axis=dim), axis, backward)
        block = jnp.concatenate([low, block, high], axis=dim)
    return block

def shards(occupancy, blur_taps, offsets, step_costs, value_start):
    ve = with_halo(value_start, (("gy", 1), ("gx", 2)), 2 * K)
    ve = jnp.pad(ve, ((0, 0), (0, 16), (0, 72 * 3 + 128 - 296)))
    v4 = jnp.stack([ve[:, :, XS * q:XS * q + 128] for q in range(NQ)], axis=1)
    oe = with_halo(occupancy.astype(jnp.bfloat16), (("gy", 0), ("gx", 1)), 2 * K + R).astype(f32)
    oe = jnp.pad(oe, ((0, 16), (0, 72 * 3 + 128 - 312)))
    occ4 = jnp.stack([oe[:, XS * q:XS * q + 128] for q in range(NQ)], axis=0)
    return call_b(offsets, step_costs, blur_taps, v4, occ4)


def solution(mesh):
    placed = (P("gy", "gx"), P(), P(), P(), P(None, "gy", "gx"))
    return jax.shard_map(shards, mesh=mesh, in_specs=placed, out_specs=(P("gy", "gx"), P(None, "gy", "gx")), check_vma=False)
```

```python
import jax, jax.numpy as jnp
from jax import lax
from jax.experimental import pallas as pl
from jax.experimental.pallas import tpu as pltpu
from jax.sharding import PartitionSpec as P

H = 16; P_SIZE = 16; K = 10; R = 8
LS = 9
NL = 32
NQ = 4
XS = 72
SE = LS + 2 * K
XE = 96
WALL = 40.0
OUT_MAP = 1e9
f32 = jnp.float32

def lane(n=8):
    return lax.broadcasted_iota(jnp.int32, (n, 128), 1)


N = 256
HV = 2 * K
HO = 2 * K + R
PER = 6
STEPS_V = (0, 8, 12)
STEPS_O = (0, 6)
i32 = jnp.int32
CODE = 65535.0 / 4.0

def code(v):
    return (v * CODE + 0.5).astype(i32)

def pair(lo, hi):
    return lo | lax.shift_left(hi, jnp.full_like(hi, 16))

def unpair(w, high):
    return lax.shift_right_logical(w, jnp.full_like(w, 16 * high)) & 0xFFFF

def value_of(w, high):
    return unpair(w, high).astype(f32) * (1.0 / CODE)

def exchange(value, occ, xh, yh, ch, vv, ov, sx, sy, sc, lsem, ssem, rsem):
    gx = lax.axis_index("gx"); gy = lax.axis_index("gy")
    nx = lax.axis_size("gx"); ny = lax.axis_size("gy")
    cols = (lax.rem(gx + nx - 1, nx), lax.rem(gx + 1, nx))
    rows = (lax.rem(gy + ny - 1, ny), lax.rem(gy + 1, ny))
    loads = [pltpu.make_async_copy(value.at[a:b], vv.at[a:b], lsem.at[n]) for n, (a, b) in enumerate(((0, 6), (6, 12), (12, 16)))]
    loads.append(pltpu.make_async_copy(occ, ov, lsem.at[3]))
    for c in loads:
        c.start()
    barrier = pltpu.get_barrier_semaphore()
    ids = [{"gx": cols[i], "gy": gy} for i in range(2)] + [{"gx": gx, "gy": rows[i]} for i in range(2)]
    ids += [{"gx": cols[i], "gy": rows[j]} for j in range(2) for i in range(2)]
    for d in ids:
        pl.semaphore_signal(barrier, inc=1, device_id=d, device_id_type=pl.DeviceIdType.MESH)
    pl.semaphore_wait(barrier, 8)
    sends = []
    def send(src, dst, d):
        n = len(sends)
        c = pltpu.make_async_remote_copy(src_ref=src, dst_ref=dst, send_sem=ssem.at[n], recv_sem=rsem.at[n], device_id=d, device_id_type=pl.DeviceIdType.MESH)
        c.start()
        sends.append(c)
    m = lane()
    loads[3].wait()
    for k in range(3):
        loads[k].wait()
        @pl.loop(0, 16)
        def _(i):
            a = pl.multiple_of(i * 8, 8)
            b = pl.multiple_of(i * 8 + 128, 8)
            for side in range(2):
                acc = jnp.zeros((8, 128), i32)
                for g in range(min(PER, H - PER * k)):
                    h = PER * k + g
                    w = pair(code(vv[h, pl.ds(a, 8), 128 * side:128 * side + 128]), code(vv[h, pl.ds(b, 8), 128 * side:128 * side + 128]))
                    w = pltpu.roll(w, (HV * g + HV * side) % 128, 1) if (g or side) else w
                    acc = jnp.where((m >= HV * g) & (m < HV * g + HV), w, acc)
                if k == 2:
                    w = pair(ov[pl.ds(a, 8), 128 * side:128 * side + 128], ov[pl.ds(b, 8), 128 * side:128 * side + 128])
                    acc = jnp.where((m >= 80) & (m < 80 + HO), pltpu.roll(w, 80 + HO * side, 1), acc)
                sx[side, k, pl.ds(a, 8), :] = acc
        for side in range(2):
            send(sx.at[side, k], xh.at[1 - side, k], ids[side])
    for v in range(2):
        @pl.loop(0, 8)
        def _(hp):
            for c in STEPS_V:
                r = c + v * (N - HV)
                for j in range(2):
                    sy[v, j, pl.ds(hp * 24 + c, 8), :] = pair(code(vv[hp, r:r + 8, 128 * j:128 * j + 128]), code(vv[hp + 8, r:r + 8, 128 * j:128 * j + 128]))
        for c in STEPS_O:
            r = c + v * (N - HO)
            for j in range(2):
                sy[v, j, 192 + c:200 + c, :] = pair(ov[r:r + 8, 128 * j:128 * j + 128], ov[r + 14:r + 22, 128 * j:128 * j + 128])
        send(sy.at[v], yh.at[1 - v], ids[2 + v])
    for v in range(2):
        for side in range(2):
            n = 2 * v + side
            for c in STEPS_V:
                acc = [jnp.zeros((8, 128), i32), jnp.zeros((8, 128), i32)]
                for hp in range(8):
                    g = hp % PER
                    w = sy[v, side, 24 * hp + c:24 * hp + c + 8, :]
                    w = pltpu.roll(w, (HV * g + HV * side) % 128, 1) if (g or side) else w
                    acc[hp // PER] = jnp.where((m >= HV * g) & (m < HV * g + HV), w, acc[hp // PER])
                sc[n, 0, c:c + 8, :] = acc[0]
                sc[n, 1, c:c + 8, :] = acc[1]
            for c in STEPS_O:
                w = pltpu.roll(sy[v, side, 192 + c:200 + c, :], 40 + HO * side, 1)
                sc[n, 1, c:c + 8, :] = jnp.where((m >= 40) & (m < 40 + HO), w, sc[n, 1, c:c + 8, :])
            send(sc.at[n], ch.at[3 - n], ids[4 + n])
    for c in sends:
        c.wait()

def halos(value, occ):
    V = pltpu.VMEM
    anyspec = pl.BlockSpec(memory_space=pl.ANY)
    return pl.pallas_call(
        exchange,
        out_shape=(jax.ShapeDtypeStruct((2, 3, 128, 128), i32), jax.ShapeDtypeStruct((2, 2, 208, 128), i32), jax.ShapeDtypeStruct((4, 2, 24, 128), i32)),
        in_specs=[anyspec, anyspec],
        out_specs=(anyspec, anyspec, anyspec),
        scratch_shapes=[V((H, N, N), f32), V((N, N), i32), V((2, 3, 128, 128), i32), V((2, 2, 208, 128), i32), V((4, 2, 24, 128), i32),
            pltpu.SemaphoreType.DMA((4,)), pltpu.SemaphoreType.DMA((12,)), pltpu.SemaphoreType.DMA((12,))],
        compiler_params=pltpu.CompilerParams(collective_id=0, has_side_effects=True, vmem_limit_bytes=16 * 2**20),
    )(value, occ)

def spread(t0, t1, lh, rh, m, first):
    a, b, d = first, (first + 128 - XS) % 128, first + 128 - 3 * XS + 128
    e = first + 128 - 2 * XS
    q0 = jnp.where(m < a, lh, pltpu.roll(t0, a, 1))
    q1 = jnp.where(m < b, pltpu.roll(t0, b, 1), pltpu.roll(t1, b, 1))
    q2 = jnp.where(m < e, pltpu.roll(t0, e, 1), pltpu.roll(t1, e, 1))
    q3 = jnp.where(m < d, pltpu.roll(t1, d, 1), rh)
    return q0, q1, q2, q3

def occupied_tiles(occ, xh, yh, ch, occ4, limits):
    r_lo, r_hi, c_lo, c_hi = limits
    m = lane()
    end = HO + 256 - 3 * XS
    def put(row, tiles):
        for q in range(NQ):
            occ4[q, pl.ds(row, 8), :] = tiles[q]
    for v in range(2):
        for high in range(2):
            for c in STEPS_O:
                t0 = unpair(yh[v, 0, 192 + c:200 + c, :], high).astype(f32)
                t1 = unpair(yh[v, 1, 192 + c:200 + c, :], high).astype(f32)
                lh = pltpu.roll(unpair(ch[2 * v, 1, c:c + 8, :], high), 88, 1).astype(f32)
                rh = pltpu.roll(unpair(ch[2 * v + 1, 1, c:c + 8, :], high), 88 + end - 128, 1).astype(f32)
                put(v * (HO + N) + 14 * high + c, spread(t0, t1, lh, rh, m, HO))
    @pl.loop(0, 16)
    def _(i):
        a = pl.multiple_of(i * 8, 8)
        wl = pltpu.roll(xh[0, 2, pl.ds(a, 8), :], 48, 1)
        wr = pltpu.roll(xh[1, 2, pl.ds(a, 8), :], 48 + end, 1)
        for high in range(2):
            r = pl.multiple_of(i * 8 + 128 * high, 8)
            t0 = occ[pl.ds(r, 8), 0:128].astype(f32)
            t1 = occ[pl.ds(r, 8), 128:256].astype(f32)
            put(r + HO, spread(t0, t1, unpair(wl, high).astype(f32), unpair(wr, high).astype(f32), m, HO))
    @pl.loop(0, 40)
    def _(i):
        row = pl.multiple_of(i * 8, 8)
        y = row + lax.broadcasted_iota(i32, (8, 128), 0) - R
        in_rows = (y >= r_lo) & (y < r_hi)
        for q in range(NQ):
            x = m + (q * XS - R)
            inside = in_rows & (x >= c_lo) & (x < c_hi)
            occ4[q, pl.ds(row, 8), :] = jnp.where(inside, occ4[q, pl.ds(row, 8), :], 0.0)

def blur(taps, occ4, vb4, ct4, mt4, cost, limits):
    r_lo, r_hi, c_lo, c_hi = limits
    src = lax.broadcasted_iota(jnp.int32, (128, 128), 0)
    dst = lax.broadcasted_iota(jnp.int32, (128, 128), 1)
    band = jnp.zeros((128, 128), f32)
    for t in range(2 * R + 1):
        band = jnp.where(src - dst == t, taps[t], band)
    @pl.loop(0, 39)
    def _(i):
        row = pl.multiple_of(i * 8, 8)
        for q in range(NQ):
            vb = taps[0] * occ4[q, pl.ds(row, 8), :]
            for t in range(1, 2 * R + 1):
                vb = vb + taps[t] * occ4[q, pl.ds(row + t, 8), :]
            vb4[q, pl.ds(row, 8), :] = vb
    for q in range(NQ):
        hb = jnp.dot(vb4[q], band, precision=lax.Precision.HIGHEST, preferred_element_type=f32)
        ct4[q] = 0.04 * hb
    @pl.loop(0, 39)
    def _(i):
        row = pl.multiple_of(i * 8, 8)
        y = row + lax.broadcasted_iota(jnp.int32, (8, 128), 0)
        in_rows = (y >= r_lo) & (y < r_hi)
        for q in range(NQ):
            x = lane() + q * XS
            inside = in_rows & (x >= c_lo) & (x < c_hi)
            mt4[q, pl.ds(row, 8), :] = jnp.where(inside, ct4[q, pl.ds(row, 8), :], OUT_MAP)
    m = lane()
    @pl.loop(0, 8)
    def _(i):
        for k in range(4):
            row = pl.multiple_of(i * 32 + k * 8, 8)
            g = [ct4[q, pl.ds(row + 20, 8), :] for q in range(NQ)]
            g = [pltpu.roll(v, s, 1) for v, s in zip(g, (108, 52, 124, 68))]
            cost[pl.ds(row, 8), 0:128] = jnp.where(m < 52, g[0], jnp.where(m < 124, g[1], g[2]))
            cost[pl.ds(row, 8), 128:256] = jnp.where(m < 68, g[2], g[3])

def aligned(x):
    return pl.multiple_of(x, 8)

def kernel_b(bases, costs, taps, start, occ, xh, yh, ch, cost, value, a1, a2, occ4, vb4, ct4, mt4, cl, vin, tmp4, st, o4, ob, vst, isem, osem):
    gx = lax.axis_index("gx"); gy = lax.axis_index("gy")
    r_lo = 20 - 256 * gy; r_hi = 20 + 256 * (lax.axis_size("gy") - gy)
    c_lo = 20 - 256 * gx; c_hi = 20 + 256 * (lax.axis_size("gx") - gx)
    def vload(t, slot):
        return pltpu.make_async_copy(start.at[t], vin.at[slot], isem.at[slot])
    vload(0, 0).start()
    occupied_tiles(occ, xh, yh, ch, occ4, (r_lo, r_hi, c_lo, c_hi))
    blur(taps, occ4, vb4, ct4, mt4, cost, (r_lo, r_hi, c_lo, c_hi))
    for s in range(LS):
        x = jnp.concatenate([mt4[q, pl.ds(s + K, NL, stride=LS), :] for q in range(NQ)], axis=0)
        cl[s] = jnp.transpose(x)[:XE]
    lanes = lane()
    end = HV + 256 - 3 * XS
    def put(slot, row, tiles):
        for q in range(NQ):
            c = mt4[q, row:row + 8, :]
            tmp4[slot, q, row:row + 8, :] = jnp.where(c > 1e8, WALL, tiles[q] + c)
    def build(slot, t):
        hp = lax.rem(t, 8)
        sh = 16 * (t // 8)
        tile = hp // PER
        g = hp - PER * tile
        back = lax.rem(128 - HV * g, 128)
        fore = lax.rem(128 + end - HV * g, 128)
        def word(w):
            return (lax.shift_right_logical(w, jnp.full_like(w, sh)) & 0xFFFF).astype(f32) * (1.0 / CODE)
        for v in range(2):
            for c in STEPS_V:
                t0 = word(yh[v, 0, pl.ds(hp * 24 + c, 8), :])
                t1 = word(yh[v, 1, pl.ds(hp * 24 + c, 8), :])
                lh = word(pltpu.roll(ch[2 * v, tile, c:c + 8, :], back, 1))
                rh = word(pltpu.roll(ch[2 * v + 1, tile, c:c + 8, :], fore, 1))
                put(slot, v * (HV + N) + c, spread(t0, t1, lh, rh, lanes, HV))
        k = t // PER
        gx_ = t - PER * k
        back = lax.rem(128 - HV * gx_, 128)
        fore = lax.rem(128 + end - HV * gx_, 128)
        for i in range(16):
            wl = pltpu.roll(xh[0, k, i * 8:i * 8 + 8, :], back, 1)
            wr = pltpu.roll(xh[1, k, i * 8:i * 8 + 8, :], fore, 1)
            for high in range(2):
                r = i * 8 + 128 * high
                put(slot, r + HV, spread(vin[slot, r:r + 8, 0:128], vin[slot, r:r + 8, 128:256], value_of(wl, high), value_of(wr, high), lanes, HV))
    vload(0, 0).wait()
    vload(1, 1).start()
    build(0, 0)
    @pl.loop(0, H)
    def _(t):
        slot = lax.rem(t, 2)
        @pl.when(t + 1 < H)
        def _():
            vload(t + 1, 1 - slot).wait()
        @pl.when(t + 2 < H)
        def _():
            vload(t + 2, slot).start()
        for s in range(SE):
            x = jnp.concatenate([tmp4[slot, q, pl.ds(s, NL, stride=LS), :] for q in range(NQ)], axis=0)
            a1[pl.ds(aligned((t * SE + s) * XE), XE), :] = jnp.transpose(x)[:XE]
        build(1 - slot, jnp.minimum(t + 1, H - 1))
    def lowest(a, h, s0):
        acc = [None] * 3
        for p in range(P_SIZE):
            base = bases[h * P_SIZE + p] + s0 * XE
            c = costs[h * P_SIZE + p]
            for u in range(3):
                v = a[pl.ds(base + u * XE, XS), :] + c
                acc[u] = v if acc[u] is None else jnp.minimum(acc[u], v)
        return acc
    def halo(h):
        h = jnp.maximum(h, 0)
        slot = lax.rem(h, 2)
        for s in range(LS):
            rows = [st[slot, s, pl.ds(r, 8), :] for r in (XS, XS + 2, K, K + 2)]
            for r, v, n in zip((0, 2, XS + K, XS + K + 2), rows, (NL, NL, 128 - NL, 128 - NL)):
                st[slot, s, pl.ds(r, 8), :] = pltpu.roll(v, n, 1)
        for s in range(LS):
            full = st[slot, s]
            def put(k, v):
                a2[pl.ds(aligned(h * (SE * XE) + k * XE), XE), :] = v
            put(s + K, full)
            put(s + K - LS, pltpu.roll(full, 1, 1))
            put(s + K + LS, pltpu.roll(full, 127, 1))
            if s == LS - 1:
                put(0, pltpu.roll(full, 2, 1))
            if s == 0:
                put(SE - 1, pltpu.roll(full, 126, 1))
    @pl.loop(0, H)
    def _(h):
        halo(h - 1)
        slot = lax.rem(h, 2)
        for s0 in range(0, LS, 3):
            acc = lowest(a1, h, s0)
            for u in range(3):
                c = cl[s0 + u, K:K + XS, :]
                st[slot, s0 + u, K:K + XS, :] = jnp.where(c > 1e8, WALL, acc[u] + c)
    halo(H - 1)
    def vstore(h, slot):
        return pltpu.make_async_copy(vst.at[slot], value.at[h], osem.at[slot])
    m = lane()
    def finish(h):
        slot = lax.rem(h, 2)
        for s in range(LS):
            x = jnp.transpose(ob[slot, s])
            for q in range(NQ):
                o4[q, pl.ds(s, NL, stride=LS), :] = x[q * NL:(q + 1) * NL]
        for i in range(32):
            v = [o4[q, pl.ds(i * 8 + K, 8), :] for q in range(NQ)]
            v = [pltpu.roll(w, n, 1) for w, n in zip(v, (118, 62, 6, 78))]
            vst[slot, i * 8:i * 8 + 8, 0:128] = jnp.where(m < 62, v[0], v[1])
            vst[slot, i * 8:i * 8 + 8, 128:256] = jnp.where(m < 6, v[1], jnp.where(m < 78, v[2], v[3]))
    @pl.loop(0, H)
    def _(h):
        prev = jnp.maximum(h - 1, 0)
        @pl.when(h >= 3)
        def _():
            vstore(h - 3, lax.rem(h - 1, 2)).wait()
        finish(prev)
        slot = lax.rem(h, 2)
        for s0 in range(0, LS, 3):
            acc = lowest(a2, h, s0)
            for u in range(3):
                ob[slot, s0 + u, 0:XS, :] = acc[u]
        @pl.when(h >= 1)
        def _():
            vstore(h - 1, lax.rem(h - 1, 2)).start()
    vstore(H - 3, 1).wait()
    finish(H - 1)
    vstore(H - 1, 1).start()
    vstore(14, 0).wait()
    vstore(15, 1).wait()

def tables(offsets, step_costs):
    h = jnp.arange(H, dtype=jnp.int32)[:, None]
    p = jnp.arange(P_SIZE, dtype=jnp.int32)[None, :]
    t = (h + p % 5 + H - 2) % H
    bases = ((t * SE + offsets[:, :, 0] + K) * XE + offsets[:, :, 1] + K).reshape(-1)
    return bases, (step_costs.astype(f32) * 0.125).reshape(-1)

def call_b(offsets, step_costs, blur_taps, start, occ, xh, yh, ch):
    S = pltpu.SMEM; V = pltpu.VMEM
    sp = lambda m: pl.BlockSpec(memory_space=m)
    bases, costs = tables(offsets, step_costs)
    return pl.pallas_call(
        kernel_b,
        out_shape=(jax.ShapeDtypeStruct((N, N), f32), jax.ShapeDtypeStruct((H, N, N), f32)),
        in_specs=[sp(S), sp(S), sp(S), sp(pl.ANY), sp(V), sp(V), sp(V), sp(V)],
        out_specs=(sp(V), sp(pl.ANY)),
        scratch_shapes=[V((H * SE * XE, 128), f32), V((H * SE * XE, 128), f32), V((NQ, 328, 128), f32), V((NQ, 312, 128), f32),
            V((NQ, 312, 128), f32), V((NQ, 312, 128), f32), V((LS, XE, 128), f32),
            V((2, N, N), f32), V((2, NQ, 312, 128), f32), V((2, LS, XE, 128), f32), V((NQ, NL * LS, 128), f32), V((2, LS, 128, 128), f32),
            V((2, N, N), f32), pltpu.SemaphoreType.DMA((2,)), pltpu.SemaphoreType.DMA((2,))],
        compiler_params=pltpu.CompilerParams(vmem_limit_bytes=63 * 2**20),
    )(bases, costs, blur_taps, start, occ, xh, yh, ch)

def shards(occupancy, blur_taps, offsets, step_costs, value_start):
    xh, yh, ch = halos(value_start, occupancy)
    return call_b(offsets, step_costs, blur_taps, value_start, occupancy, xh, yh, ch)


def solution(mesh):
    placed = (P("gy", "gx"), P(), P(), P(), P(None, "gy", "gx"))
    return jax.shard_map(shards, mesh=mesh, in_specs=placed, out_specs=(P("gy", "gx"), P(None, "gy", "gx")), check_vma=False)
```

```python
import jax, jax.numpy as jnp
from jax import lax
from jax.experimental import pallas as pl
from jax.experimental.pallas import tpu as pltpu
from jax.sharding import PartitionSpec as P

H = 16; P_SIZE = 16; K = 10; R = 8
LS = 9
NL = 32
NQ = 4
XS = 72
SE = LS + 2 * K
XE = 96
WALL = 40.0
OUT_MAP = 1e9
f32 = jnp.float32

def lane(n=8):
    return lax.broadcasted_iota(jnp.int32, (n, 128), 1)


N = 256
HV = 2 * K
HO = 2 * K + R
PER = 6
STEPS_V = (0, 8, 12)
STEPS_O = (0, 6)
i32 = jnp.int32
MX = 99
CODE = 65535.0 / 4.0

def code(v):
    return (v * CODE + 0.5).astype(i32)

def pair(lo, hi):
    return lo | lax.shift_left(hi, jnp.full_like(hi, 16))

def unpair(w, high):
    return lax.shift_right_logical(w, jnp.full_like(w, 16 * high)) & 0xFFFF

def value_of(w, high):
    return unpair(w, high).astype(f32) * (1.0 / CODE)

def exchange(offs, costs, value, occ, xh, yh, ch, bases, cost8, vv, ov, sx, sy, sc, lsem, ssem, rsem):
    gx = lax.axis_index("gx"); gy = lax.axis_index("gy")
    nx = lax.axis_size("gx"); ny = lax.axis_size("gy")
    cols = (lax.rem(gx + nx - 1, nx), lax.rem(gx + 1, nx))
    rows = (lax.rem(gy + ny - 1, ny), lax.rem(gy + 1, ny))
    loads = [pltpu.make_async_copy(value.at[a:b], vv.at[a:b], lsem.at[n]) for n, (a, b) in enumerate(((0, 6), (6, 12), (12, 16)))]
    loads.append(pltpu.make_async_copy(occ, ov, lsem.at[3]))
    for c in loads:
        c.start()
    barrier = pltpu.get_barrier_semaphore()
    ids = [{"gx": cols[i], "gy": gy} for i in range(2)] + [{"gx": gx, "gy": rows[i]} for i in range(2)]
    ids += [{"gx": cols[i], "gy": rows[j]} for j in range(2) for i in range(2)]
    for d in ids:
        pl.semaphore_signal(barrier, inc=1, device_id=d, device_id_type=pl.DeviceIdType.MESH)
    pl.semaphore_wait(barrier, 8)
    sends = []
    def send(src, dst, d):
        n = len(sends)
        c = pltpu.make_async_remote_copy(src_ref=src, dst_ref=dst, send_sem=ssem.at[n], recv_sem=rsem.at[n], device_id=d, device_id_type=pl.DeviceIdType.MESH)
        c.start()
        sends.append(c)
    m = lane()
    loads[3].wait()
    for k in range(3):
        loads[k].wait()
        @pl.loop(0, 16)
        def _(i):
            a = pl.multiple_of(i * 8, 8)
            b = pl.multiple_of(i * 8 + 128, 8)
            for side in range(2):
                acc = jnp.zeros((8, 128), i32)
                for g in range(min(PER, H - PER * k)):
                    h = PER * k + g
                    w = pair(code(vv[h, pl.ds(a, 8), 128 * side:128 * side + 128]), code(vv[h, pl.ds(b, 8), 128 * side:128 * side + 128]))
                    w = pltpu.roll(w, (HV * g + HV * side) % 128, 1) if (g or side) else w
                    acc = jnp.where((m >= HV * g) & (m < HV * g + HV), w, acc)
                if k == 2:
                    w = pair(ov[pl.ds(a, 8), 128 * side:128 * side + 128], ov[pl.ds(b, 8), 128 * side:128 * side + 128])
                    acc = jnp.where((m >= 80) & (m < 80 + HO), pltpu.roll(w, 80 + HO * side, 1), acc)
                sx[side, k, pl.ds(a, 8), :] = acc
        for side in range(2):
            send(sx.at[side, k], xh.at[1 - side, k], ids[side])
    for v in range(2):
        @pl.loop(0, 8)
        def _(hp):
            for c in STEPS_V:
                r = c + v * (N - HV)
                for j in range(2):
                    sy[v, j, pl.ds(hp * 24 + c, 8), :] = pair(code(vv[hp, r:r + 8, 128 * j:128 * j + 128]), code(vv[hp + 8, r:r + 8, 128 * j:128 * j + 128]))
        for c in STEPS_O:
            r = c + v * (N - HO)
            for j in range(2):
                sy[v, j, 192 + c:200 + c, :] = pair(ov[r:r + 8, 128 * j:128 * j + 128], ov[r + 14:r + 22, 128 * j:128 * j + 128])
        send(sy.at[v], yh.at[1 - v], ids[2 + v])
    for v in range(2):
        for side in range(2):
            n = 2 * v + side
            for c in STEPS_V:
                acc = [jnp.zeros((8, 128), i32), jnp.zeros((8, 128), i32)]
                for hp in range(8):
                    g = hp % PER
                    w = sy[v, side, 24 * hp + c:24 * hp + c + 8, :]
                    w = pltpu.roll(w, (HV * g + HV * side) % 128, 1) if (g or side) else w
                    acc[hp // PER] = jnp.where((m >= HV * g) & (m < HV * g + HV), w, acc[hp // PER])
                sc[n, 0, c:c + 8, :] = acc[0]
                sc[n, 1, c:c + 8, :] = acc[1]
            for c in STEPS_O:
                w = pltpu.roll(sy[v, side, 192 + c:200 + c, :], 40 + HO * side, 1)
                sc[n, 1, c:c + 8, :] = jnp.where((m >= 40) & (m < 40 + HO), w, sc[n, 1, c:c + 8, :])
            send(sc.at[n], ch.at[3 - n], ids[4 + n])
    @pl.loop(0, H)
    def _(h):
        for p in range(P_SIZE):
            n = h * P_SIZE + p
            t = lax.rem(h + (p % 5 + H - 2), H)
            bases[n] = (t * SE + offs[h, p, 0] + K) * XE + offs[h, p, 1] + K
            cost8[n] = costs[h, p].astype(f32) * 0.125
    for c in sends:
        c.wait()

def halos(offsets, step_costs, value, occ):
    V = pltpu.VMEM
    anyspec = pl.BlockSpec(memory_space=pl.ANY)
    smem = pl.BlockSpec(memory_space=pltpu.SMEM)
    return pl.pallas_call(
        exchange,
        out_shape=(jax.ShapeDtypeStruct((2, 3, 128, 128), i32), jax.ShapeDtypeStruct((2, 2, 208, 128), i32), jax.ShapeDtypeStruct((4, 2, 24, 128), i32),
            jax.ShapeDtypeStruct((H * P_SIZE,), i32), jax.ShapeDtypeStruct((H * P_SIZE,), f32)),
        in_specs=[smem, smem, anyspec, anyspec],
        out_specs=(anyspec, anyspec, anyspec, smem, smem),
        scratch_shapes=[V((H, N, N), f32), V((N, N), i32), V((2, 3, 128, 128), i32), V((2, 2, 208, 128), i32), V((4, 2, 24, 128), i32),
            pltpu.SemaphoreType.DMA((4,)), pltpu.SemaphoreType.DMA((12,)), pltpu.SemaphoreType.DMA((12,))],
        compiler_params=pltpu.CompilerParams(collective_id=0, has_side_effects=True, vmem_limit_bytes=63 * 2**20),
    )(offsets, step_costs, value, occ)

def spread(t0, t1, lh, rh, m, first):
    a, b, d = first, (first + 128 - XS) % 128, first + 128 - 3 * XS + 128
    e = first + 128 - 2 * XS
    q0 = jnp.where(m < a, lh, pltpu.roll(t0, a, 1))
    q1 = jnp.where(m < b, pltpu.roll(t0, b, 1), pltpu.roll(t1, b, 1))
    q2 = jnp.where(m < e, pltpu.roll(t0, e, 1), pltpu.roll(t1, e, 1))
    q3 = jnp.where(m < d, pltpu.roll(t1, d, 1), rh)
    return q0, q1, q2, q3

def occupied_tiles(occ, xh, yh, ch, occ4, limits):
    r_lo, r_hi, c_lo, c_hi = limits
    m = lane()
    end = HO + 256 - 3 * XS
    def put(row, tiles):
        for q in range(NQ):
            occ4[q, pl.ds(row, 8), :] = tiles[q]
    for v in range(2):
        for high in range(2):
            for c in STEPS_O:
                t0 = unpair(yh[v, 0, 192 + c:200 + c, :], high).astype(f32)
                t1 = unpair(yh[v, 1, 192 + c:200 + c, :], high).astype(f32)
                lh = pltpu.roll(unpair(ch[2 * v, 1, c:c + 8, :], high), 88, 1).astype(f32)
                rh = pltpu.roll(unpair(ch[2 * v + 1, 1, c:c + 8, :], high), 88 + end - 128, 1).astype(f32)
                put(v * (HO + N) + 14 * high + c, spread(t0, t1, lh, rh, m, HO))
    @pl.loop(0, 16)
    def _(i):
        a = pl.multiple_of(i * 8, 8)
        wl = pltpu.roll(xh[0, 2, pl.ds(a, 8), :], 48, 1)
        wr = pltpu.roll(xh[1, 2, pl.ds(a, 8), :], 48 + end, 1)
        for high in range(2):
            r = pl.multiple_of(i * 8 + 128 * high, 8)
            t0 = occ[pl.ds(r, 8), 0:128].astype(f32)
            t1 = occ[pl.ds(r, 8), 128:256].astype(f32)
            put(r + HO, spread(t0, t1, unpair(wl, high).astype(f32), unpair(wr, high).astype(f32), m, HO))
    @pl.loop(0, 40)
    def _(i):
        row = pl.multiple_of(i * 8, 8)
        y = row + lax.broadcasted_iota(i32, (8, 128), 0) - R
        in_rows = (y >= r_lo) & (y < r_hi)
        for q in range(NQ):
            x = m + (q * XS - R)
            inside = in_rows & (x >= c_lo) & (x < c_hi)
            occ4[q, pl.ds(row, 8), :] = jnp.where(inside, occ4[q, pl.ds(row, 8), :], 0.0)

def blur(taps, occ4, vb4, ct4, mt4, cost, limits):
    r_lo, r_hi, c_lo, c_hi = limits
    src = lax.broadcasted_iota(jnp.int32, (128, 128), 0)
    dst = lax.broadcasted_iota(jnp.int32, (128, 128), 1)
    band = jnp.zeros((128, 128), f32)
    for t in range(2 * R + 1):
        band = jnp.where(src - dst == t, taps[t], band)
    @pl.loop(0, 39)
    def _(i):
        row = pl.multiple_of(i * 8, 8)
        for q in range(NQ):
            vb = taps[0] * occ4[q, pl.ds(row, 8), :]
            for t in range(1, 2 * R + 1):
                vb = vb + taps[t] * occ4[q, pl.ds(row + t, 8), :]
            vb4[q, pl.ds(row, 8), :] = vb
    b16 = jnp.bfloat16
    band_hi = band.astype(b16)
    band_lo = (band - band_hi.astype(f32)).astype(b16)
    @pl.loop(0, 3)
    def _(i):
        row = pl.multiple_of(i * 104, 8)
        for q in range(NQ):
            v = vb4[q, pl.ds(row, 104), :]
            v_hi = v.astype(b16)
            v_lo = (v - v_hi.astype(f32)).astype(b16)
            dot = lambda x, y: jnp.dot(x, y, preferred_element_type=f32)
            ct4[q, pl.ds(row, 104), :] = 0.04 * (dot(v_hi, band_hi) + (dot(v_hi, band_lo) + dot(v_lo, band_hi)))
    @pl.loop(0, 39)
    def _(i):
        row = pl.multiple_of(i * 8, 8)
        y = row + lax.broadcasted_iota(jnp.int32, (8, 128), 0)
        in_rows = (y >= r_lo) & (y < r_hi)
        for q in range(NQ):
            x = lane() + q * XS
            inside = in_rows & (x >= c_lo) & (x < c_hi)
            mt4[q, pl.ds(row, 8), :] = jnp.where(inside, ct4[q, pl.ds(row, 8), :], OUT_MAP)
    m = lane()
    @pl.loop(0, 8)
    def _(i):
        for k in range(4):
            row = pl.multiple_of(i * 32 + k * 8, 8)
            g = [ct4[q, pl.ds(row + 20, 8), :] for q in range(NQ)]
            g = [pltpu.roll(v, s, 1) for v, s in zip(g, (108, 52, 124, 68))]
            cost[pl.ds(row, 8), 0:128] = jnp.where(m < 52, g[0], jnp.where(m < 124, g[1], g[2]))
            cost[pl.ds(row, 8), 128:256] = jnp.where(m < 68, g[2], g[3])

def aligned(x):
    return pl.multiple_of(x, 8)

def kernel_b(bases, costs, taps, start, occ_in, xh_in, yh_in, ch_in, cost, value, a1, a2, occ4, vb4, ct4, mt4, cl, vin, tmp_a, tmp_b, st, o4, ob, vst, occ, xh, yh, ch, pick, lhs, isem, osem, hsem):
    gx = lax.axis_index("gx"); gy = lax.axis_index("gy")
    r_lo = 20 - 256 * gy; r_hi = 20 + 256 * (lax.axis_size("gy") - gy)
    c_lo = 20 - 256 * gx; c_hi = 20 + 256 * (lax.axis_size("gx") - gx)
    def vload(t, slot):
        return pltpu.make_async_copy(start.at[t], vin.at[slot], isem.at[slot])
    halo_loads = [pltpu.make_async_copy(x, y, hsem.at[n]) for n, (x, y) in enumerate(((occ_in, occ), (xh_in, xh), (yh_in, yh), (ch_in, ch)))]
    for c in halo_loads:
        c.start()
    vload(0, 0).start()
    for c in halo_loads:
        c.wait()
    occupied_tiles(occ, xh, yh, ch, occ4, (r_lo, r_hi, c_lo, c_hi))
    blur(taps, occ4, vb4, ct4, mt4, cost, (r_lo, r_hi, c_lo, c_hi))
    for s in range(LS):
        x = jnp.concatenate([mt4[q, pl.ds(s + K, NL, stride=LS), :] for q in range(NQ)], axis=0)
        cl[s] = jnp.transpose(x)[:XE]
    end = HV + 256 - 3 * XS
    b16 = jnp.bfloat16
    for j in range(2):
        src = lax.broadcasted_iota(i32, (256, 512), 0)
        dst = lax.broadcasted_iota(i32, (256, 512), 1)
        pick[256 * j:256 * j + 256, :] = jnp.where(src == (dst // 128) * XS + lax.rem(dst, 128) - HV, 1.0, 0.0).astype(b16)
    def build(tmp, slot, t):
        hp = lax.rem(t, 8)
        sh = 16 * (t // 8)
        tile = hp // PER
        g = hp - PER * tile
        back = lax.rem(128 - HV * g, 128)
        fore = lax.rem(128 + end - HV * g, 128)
        def word(w):
            return (lax.shift_right_logical(w, jnp.full_like(w, sh)) & 0xFFFF).astype(f32) * (1.0 / CODE)
        def parts(row, v):
            n = v.shape[0]
            hi = v.astype(b16)
            lhs[row:row + n, 0:256] = hi
            lhs[row:row + n, 256:512] = (v - hi.astype(f32)).astype(b16)
        def put(rows, row, v, lh, rh):
            m = lane(rows)
            v[0] = jnp.where(m < HV, lh, v[0])
            v[3] = jnp.where(m < end, v[3], rh)
            for q in range(NQ):
                c = mt4[q, row:row + rows, :]
                tmp[q, row:row + rows, :] = jnp.where(c > 1e8, WALL, v[q] + c)
        k = t // PER
        gk = t - PER * k
        backk = lax.rem(128 - HV * gk, 128)
        forek = lax.rem(128 + end - HV * gk, 128)
        parts(0, vin[slot])
        parts(256, jnp.concatenate([jnp.concatenate([word(yh[v, j, pl.ds(hp * 24 + c, 8), :]) for j in range(2)], axis=1)
            for v in range(2) for c in STEPS_V], axis=0))
        o = jnp.dot(lhs[...], pick[...], preferred_element_type=f32)
        o = [o[:, 128 * q:128 * q + 128] for q in range(NQ)]
        for i in range(2):
            wl = pltpu.roll(xh[0, k, i * 64:i * 64 + 64, :], backk, 1)
            wr = pltpu.roll(xh[1, k, i * 64:i * 64 + 64, :], forek, 1)
            for high in range(2):
                r = i * 64 + 128 * high
                put(64, r + HV, [e[r:r + 64] for e in o], value_of(wl, high), value_of(wr, high))
        n = 256
        for v in range(2):
            for c in STEPS_V:
                lh = word(pltpu.roll(ch[2 * v, tile, c:c + 8, :], back, 1))
                rh = word(pltpu.roll(ch[2 * v + 1, tile, c:c + 8, :], fore, 1))
                put(8, v * (HV + N) + c, [e[n:n + 8] for e in o], lh, rh)
                n += 8
    vload(0, 0).wait()
    vload(1, 1).start()
    build(tmp_a, 0, 0)
    ri = lax.broadcasted_iota(i32, (XE, 256), 0)
    ci = lax.broadcasted_iota(i32, (XE, 256), 1)
    eye = jnp.where((ri == ci) | (ri + 128 == ci), 1.0, 0.0).astype(b16)
    def turn(tmp, t):
        for s in range(SE):
            x = jnp.concatenate([tmp[q, pl.ds(s, NL, stride=LS), :] for q in range(NQ)], axis=0)
            if s % MX == MX - 1:
                hi = x.astype(b16)
                lo = (x - hi.astype(f32)).astype(b16)
                y = lax.dot_general(eye, jnp.concatenate([hi, lo], axis=1), (((1,), (1,)), ((), ())), preferred_element_type=f32)
            else:
                y = jnp.transpose(x)[:XE]
            a1[pl.ds(aligned((t * SE + s) * XE), XE), :] = y
    @pl.loop(0, H // 2)
    def _(i):
        t = 2 * i
        vload(t + 1, 1).wait()
        @pl.when(i < H // 2 - 1)
        def _():
            vload(t + 2, 0).start()
        build(tmp_b, 1, t + 1)
        turn(tmp_a, t)
        @pl.when(i < H // 2 - 1)
        def _():
            vload(t + 2, 0).wait()
            vload(t + 3, 1).start()
        build(tmp_a, 0, jnp.minimum(t + 2, H - 1))
        turn(tmp_b, t + 1)
    def lowest(a, h, s0):
        acc = [None] * 3
        for p in range(P_SIZE):
            base = bases[h * P_SIZE + p] + s0 * XE
            c = costs[h * P_SIZE + p]
            for u in range(3):
                v = a[pl.ds(base + u * XE, XS), :] + c
                acc[u] = v if acc[u] is None else jnp.minimum(acc[u], v)
        return acc
    def halo(h):
        h = jnp.maximum(h, 0)
        slot = lax.rem(h, 2)
        for s in range(LS):
            rows = [st[slot, s, pl.ds(r, 8), :] for r in (XS, XS + 2, K, K + 2)]
            for r, v, n in zip((0, 2, XS + K, XS + K + 2), rows, (NL, NL, 128 - NL, 128 - NL)):
                st[slot, s, pl.ds(r, 8), :] = pltpu.roll(v, n, 1)
        for s in range(LS):
            full = st[slot, s]
            def put(k, v):
                a2[pl.ds(aligned(h * (SE * XE) + k * XE), XE), :] = v
            put(s + K, full)
            put(s + K - LS, pltpu.roll(full, 1, 1))
            put(s + K + LS, pltpu.roll(full, 127, 1))
            if s == LS - 1:
                put(0, pltpu.roll(full, 2, 1))
            if s == 0:
                put(SE - 1, pltpu.roll(full, 126, 1))
    @pl.loop(0, H)
    def _(h):
        halo(h - 1)
        slot = lax.rem(h, 2)
        for s0 in range(0, LS, 3):
            acc = lowest(a1, h, s0)
            for u in range(3):
                c = cl[s0 + u, K:K + XS, :]
                st[slot, s0 + u, K:K + XS, :] = jnp.where(c > 1e8, WALL, acc[u] + c)
    halo(H - 1)
    def vstore(h):
        return pltpu.make_async_copy(vst.at[lax.rem(h, 2)], value.at[h], osem.at[lax.rem(h, 2)])
    m = lane()
    def back(h):
        slot = lax.rem(h, 2)
        for s in range(LS):
            x = jnp.transpose(ob[slot, s])
            for q in range(NQ):
                o4[slot, q, pl.ds(s, NL, stride=LS), :] = x[q * NL:(q + 1) * NL]
    def assemble(h):
        slot = lax.rem(h, 2)
        for i in range(32):
            v = [o4[slot, q, pl.ds(i * 8 + K, 8), :] for q in range(NQ)]
            v = [pltpu.roll(w, n, 1) for w, n in zip(v, (118, 62, 6, 78))]
            vst[slot, i * 8:i * 8 + 8, 0:128] = jnp.where(m < 62, v[0], v[1])
            vst[slot, i * 8:i * 8 + 8, 128:256] = jnp.where(m < 6, v[1], jnp.where(m < 78, v[2], v[3]))
    @pl.loop(0, H)
    def _(h):
        @pl.when(h >= 4)
        def _():
            vstore(h - 4).wait()
        assemble(lax.rem(h, 2))
        back(lax.rem(h + 1, 2))
        slot = lax.rem(h, 2)
        for s0 in range(0, LS, 3):
            acc = lowest(a2, h, s0)
            for u in range(3):
                ob[slot, s0 + u, 0:XS, :] = acc[u]
        @pl.when(h >= 2)
        def _():
            vstore(h - 2).start()
    for h in (H, H + 1):
        vstore(h - 4).wait()
        assemble(h - 2)
        vstore(h - 2).start()
        if h == H:
            back(h - 1)
    vstore(H - 2).wait()
    vstore(H - 1).wait()

def call_b(bases, costs, blur_taps, start, occ, xh, yh, ch):
    S = pltpu.SMEM; V = pltpu.VMEM
    sp = lambda m: pl.BlockSpec(memory_space=m)
    return pl.pallas_call(
        kernel_b,
        out_shape=(jax.ShapeDtypeStruct((N, N), f32), jax.ShapeDtypeStruct((H, N, N), f32)),
        in_specs=[sp(S), sp(S), sp(S)] + [sp(pl.ANY)] * 5,
        out_specs=(sp(V), sp(pl.ANY)),
        scratch_shapes=[V((H * SE * XE, 128), f32), V((H * SE * XE, 128), f32), V((NQ, 328, 128), f32), V((NQ, 312, 128), f32),
            V((NQ, 312, 128), f32), V((NQ, 312, 128), f32), V((LS, XE, 128), f32),
            V((2, N, N), f32), V((NQ, 312, 128), f32), V((NQ, 312, 128), f32), V((2, LS, XE, 128), f32), V((2, NQ, NL * LS, 128), f32), V((2, LS, 128, 128), f32),
            V((2, N, N), f32), V((N, N), i32), V((2, 3, 128, 128), i32), V((2, 2, 208, 128), i32), V((4, 2, 24, 128), i32), V((512, 512), jnp.bfloat16), V((304, 512), jnp.bfloat16),
            pltpu.SemaphoreType.DMA((2,)), pltpu.SemaphoreType.DMA((2,)), pltpu.SemaphoreType.DMA((4,))],
        compiler_params=pltpu.CompilerParams(vmem_limit_bytes=63 * 2**20),
    )(bases, costs, blur_taps, start, occ, xh, yh, ch)

def shards(occupancy, blur_taps, offsets, step_costs, value_start):
    xh, yh, ch, bases, costs = halos(offsets, step_costs, value_start, occupancy)
    return call_b(bases, costs, blur_taps, value_start, occupancy, xh, yh, ch)


def solution(mesh):
    placed = (P("gy", "gx"), P(), P(), P(), P(None, "gy", "gx"))
    return jax.shard_map(shards, mesh=mesh, in_specs=placed, out_specs=(P("gy", "gx"), P(None, "gy", "gx")), check_vma=False)
```

```python
import jax, jax.numpy as jnp
from jax import lax
from jax.experimental import pallas as pl
from jax.experimental.pallas import tpu as pltpu
from jax.sharding import PartitionSpec as P

H = 16; P_SIZE = 16; K = 10; R = 8
LS = 9
NL = 32
NQ = 4
XS = 72
SE = LS + 2 * K
XE = 96
WALL = 40.0
OUT_MAP = 1e9
f32 = jnp.float32

def lane(n=8):
    return lax.broadcasted_iota(jnp.int32, (n, 128), 1)


N = 256
HV = 2 * K
HO = 2 * K + R
PER = 6
STEPS_V = (0, 8, 12)
STEPS_O = (0, 6)
i32 = jnp.int32
MX = 3
CODE = 65535.0 / 4.0

def code(v):
    return (v * CODE + 0.5).astype(i32)

def pair(lo, hi):
    return lo | lax.shift_left(hi, jnp.full_like(hi, 16))

def unpair(w, high):
    return lax.shift_right_logical(w, jnp.full_like(w, 16 * high)) & 0xFFFF

def value_of(w, high):
    return unpair(w, high).astype(f32) * (1.0 / CODE)

def exchange(offs, costs, value, occ, xh, yh, ch, bases, cost8, vv, ov, sx, sy, sc, lsem, ssem, rsem):
    gx = lax.axis_index("gx"); gy = lax.axis_index("gy")
    nx = lax.axis_size("gx"); ny = lax.axis_size("gy")
    cols = (lax.rem(gx + nx - 1, nx), lax.rem(gx + 1, nx))
    rows = (lax.rem(gy + ny - 1, ny), lax.rem(gy + 1, ny))
    loads = [pltpu.make_async_copy(value.at[a:b], vv.at[a:b], lsem.at[n]) for n, (a, b) in enumerate(((0, 6), (6, 12), (12, 16)))]
    loads.append(pltpu.make_async_copy(occ, ov, lsem.at[3]))
    for c in loads:
        c.start()
    barrier = pltpu.get_barrier_semaphore()
    ids = [{"gx": cols[i], "gy": gy} for i in range(2)] + [{"gx": gx, "gy": rows[i]} for i in range(2)]
    ids += [{"gx": cols[i], "gy": rows[j]} for j in range(2) for i in range(2)]
    for d in ids:
        pl.semaphore_signal(barrier, inc=1, device_id=d, device_id_type=pl.DeviceIdType.MESH)
    sends = []
    def send(src, dst, d):
        n = len(sends)
        c = pltpu.make_async_remote_copy(src_ref=src, dst_ref=dst, send_sem=ssem.at[n], recv_sem=rsem.at[n], device_id=d, device_id_type=pl.DeviceIdType.MESH)
        c.start()
        sends.append(c)
    m = lane()
    loads[3].wait()
    for k in range(3):
        loads[k].wait()
        @pl.loop(0, 16)
        def _(i):
            a = pl.multiple_of(i * 8, 8)
            b = pl.multiple_of(i * 8 + 128, 8)
            for side in range(2):
                acc = jnp.zeros((8, 128), i32)
                for g in range(min(PER, H - PER * k)):
                    h = PER * k + g
                    w = pair(code(vv[h, pl.ds(a, 8), 128 * side:128 * side + 128]), code(vv[h, pl.ds(b, 8), 128 * side:128 * side + 128]))
                    w = pltpu.roll(w, (HV * g + HV * side) % 128, 1) if (g or side) else w
                    acc = jnp.where((m >= HV * g) & (m < HV * g + HV), w, acc)
                if k == 2:
                    w = pair(ov[pl.ds(a, 8), 128 * side:128 * side + 128], ov[pl.ds(b, 8), 128 * side:128 * side + 128])
                    acc = jnp.where((m >= 80) & (m < 80 + HO), pltpu.roll(w, 80 + HO * side, 1), acc)
                sx[side, k, pl.ds(a, 8), :] = acc
        if k == 0:
            pl.semaphore_wait(barrier, 8)
        for side in range(2):
            send(sx.at[side, k], xh.at[1 - side, k], ids[side])
    for v in range(2):
        @pl.loop(0, 8)
        def _(hp):
            for c in STEPS_V:
                r = c + v * (N - HV)
                for j in range(2):
                    sy[v, j, pl.ds(hp * 24 + c, 8), :] = pair(code(vv[hp, r:r + 8, 128 * j:128 * j + 128]), code(vv[hp + 8, r:r + 8, 128 * j:128 * j + 128]))
        for c in STEPS_O:
            r = c + v * (N - HO)
            for j in range(2):
                sy[v, j, 192 + c:200 + c, :] = pair(ov[r:r + 8, 128 * j:128 * j + 128], ov[r + 14:r + 22, 128 * j:128 * j + 128])
        send(sy.at[v], yh.at[1 - v], ids[2 + v])
    for v in range(2):
        for side in range(2):
            n = 2 * v + side
            for c in STEPS_V:
                acc = [jnp.zeros((8, 128), i32), jnp.zeros((8, 128), i32)]
                for hp in range(8):
                    g = hp % PER
                    w = sy[v, side, 24 * hp + c:24 * hp + c + 8, :]
                    w = pltpu.roll(w, (HV * g + HV * side) % 128, 1) if (g or side) else w
                    acc[hp // PER] = jnp.where((m >= HV * g) & (m < HV * g + HV), w, acc[hp // PER])
                sc[n, 0, c:c + 8, :] = acc[0]
                sc[n, 1, c:c + 8, :] = acc[1]
            for c in STEPS_O:
                w = pltpu.roll(sy[v, side, 192 + c:200 + c, :], 40 + HO * side, 1)
                sc[n, 1, c:c + 8, :] = jnp.where((m >= 40) & (m < 40 + HO), w, sc[n, 1, c:c + 8, :])
            send(sc.at[n], ch.at[3 - n], ids[4 + n])
    @pl.loop(0, H)
    def _(h):
        for p in range(P_SIZE):
            n = h * P_SIZE + p
            t = lax.rem(h + (p % 5 + H - 2), H)
            bases[n] = t * (SE * XE) + offs[h, p]
            cost8[n] = costs[h, p].astype(f32) * 0.125
    for c in sends:
        c.wait()

def halos(offsets, step_costs, value, occ):
    V = pltpu.VMEM
    anyspec = pl.BlockSpec(memory_space=pl.ANY)
    smem = pl.BlockSpec(memory_space=pltpu.SMEM)
    return pl.pallas_call(
        exchange,
        out_shape=(jax.ShapeDtypeStruct((2, 3, 128, 128), i32), jax.ShapeDtypeStruct((2, 2, 208, 128), i32), jax.ShapeDtypeStruct((4, 2, 24, 128), i32),
            jax.ShapeDtypeStruct((H * P_SIZE,), i32), jax.ShapeDtypeStruct((H * P_SIZE,), f32)),
        in_specs=[smem, smem, anyspec, anyspec],
        out_specs=(anyspec, anyspec, anyspec, smem, smem),
        scratch_shapes=[V((H, N, N), f32), V((N, N), i32), V((2, 3, 128, 128), i32), V((2, 2, 208, 128), i32), V((4, 2, 24, 128), i32),
            pltpu.SemaphoreType.DMA((4,)), pltpu.SemaphoreType.DMA((12,)), pltpu.SemaphoreType.DMA((12,))],
        compiler_params=pltpu.CompilerParams(collective_id=0, has_side_effects=True, vmem_limit_bytes=63 * 2**20),
    )(offsets, step_costs, value, occ)

def spread(t0, t1, lh, rh, m, first):
    a, b, d = first, (first + 128 - XS) % 128, first + 128 - 3 * XS + 128
    e = first + 128 - 2 * XS
    q0 = jnp.where(m < a, lh, pltpu.roll(t0, a, 1))
    q1 = jnp.where(m < b, pltpu.roll(t0, b, 1), pltpu.roll(t1, b, 1))
    q2 = jnp.where(m < e, pltpu.roll(t0, e, 1), pltpu.roll(t1, e, 1))
    q3 = jnp.where(m < d, pltpu.roll(t1, d, 1), rh)
    return q0, q1, q2, q3

def occupied_tiles(occ, xh, yh, ch, occ4, limits):
    r_lo, r_hi, c_lo, c_hi = limits
    m = lane()
    end = HO + 256 - 3 * XS
    def put(row, tiles):
        for q in range(NQ):
            occ4[q, pl.ds(row, 8), :] = tiles[q]
    for v in range(2):
        for high in range(2):
            for c in STEPS_O:
                t0 = unpair(yh[v, 0, 192 + c:200 + c, :], high).astype(f32)
                t1 = unpair(yh[v, 1, 192 + c:200 + c, :], high).astype(f32)
                lh = pltpu.roll(unpair(ch[2 * v, 1, c:c + 8, :], high), 88, 1).astype(f32)
                rh = pltpu.roll(unpair(ch[2 * v + 1, 1, c:c + 8, :], high), 88 + end - 128, 1).astype(f32)
                put(v * (HO + N) + 14 * high + c, spread(t0, t1, lh, rh, m, HO))
    @pl.loop(0, 16)
    def _(i):
        a = pl.multiple_of(i * 8, 8)
        wl = pltpu.roll(xh[0, 2, pl.ds(a, 8), :], 48, 1)
        wr = pltpu.roll(xh[1, 2, pl.ds(a, 8), :], 48 + end, 1)
        for high in range(2):
            r = pl.multiple_of(i * 8 + 128 * high, 8)
            t0 = occ[pl.ds(r, 8), 0:128].astype(f32)
            t1 = occ[pl.ds(r, 8), 128:256].astype(f32)
            put(r + HO, spread(t0, t1, unpair(wl, high).astype(f32), unpair(wr, high).astype(f32), m, HO))
    @pl.loop(0, 40)
    def _(i):
        row = pl.multiple_of(i * 8, 8)
        y = row + lax.broadcasted_iota(i32, (8, 128), 0) - R
        in_rows = (y >= r_lo) & (y < r_hi)
        for q in range(NQ):
            x = m + (q * XS - R)
            inside = in_rows & (x >= c_lo) & (x < c_hi)
            occ4[q, pl.ds(row, 8), :] = jnp.where(inside, occ4[q, pl.ds(row, 8), :], 0.0)

def blur(taps, occ4, vb4, ct4, mt4, cost, limits):
    r_lo, r_hi, c_lo, c_hi = limits
    src = lax.broadcasted_iota(jnp.int32, (128, 128), 0)
    dst = lax.broadcasted_iota(jnp.int32, (128, 128), 1)
    band = jnp.zeros((128, 128), f32)
    for t in range(2 * R + 1):
        band = jnp.where(src - dst == t, taps[t], band)
    @pl.loop(0, 39)
    def _(i):
        row = pl.multiple_of(i * 8, 8)
        for q in range(NQ):
            vb = taps[0] * occ4[q, pl.ds(row, 8), :]
            for t in range(1, 2 * R + 1):
                vb = vb + taps[t] * occ4[q, pl.ds(row + t, 8), :]
            vb4[q, pl.ds(row, 8), :] = vb
    b16 = jnp.bfloat16
    band_hi = band.astype(b16)
    band_lo = (band - band_hi.astype(f32)).astype(b16)
    @pl.loop(0, 3)
    def _(i):
        row = pl.multiple_of(i * 104, 8)
        for q in range(NQ):
            v = vb4[q, pl.ds(row, 104), :]
            v_hi = v.astype(b16)
            v_lo = (v - v_hi.astype(f32)).astype(b16)
            dot = lambda x, y: jnp.dot(x, y, preferred_element_type=f32)
            ct4[q, pl.ds(row, 104), :] = 0.04 * (dot(v_hi, band_hi) + (dot(v_hi, band_lo) + dot(v_lo, band_hi)))
    @pl.loop(0, 39)
    def _(i):
        row = pl.multiple_of(i * 8, 8)
        y = row + lax.broadcasted_iota(jnp.int32, (8, 128), 0)
        in_rows = (y >= r_lo) & (y < r_hi)
        for q in range(NQ):
            x = lane() + q * XS
            inside = in_rows & (x >= c_lo) & (x < c_hi)
            mt4[q, pl.ds(row, 8), :] = jnp.where(inside, ct4[q, pl.ds(row, 8), :], OUT_MAP)
    m = lane()
    @pl.loop(0, 8)
    def _(i):
        for k in range(4):
            row = pl.multiple_of(i * 32 + k * 8, 8)
            g = [ct4[q, pl.ds(row + 20, 8), :] for q in range(NQ)]
            g = [pltpu.roll(v, s, 1) for v, s in zip(g, (108, 52, 124, 68))]
            cost[pl.ds(row, 8), 0:128] = jnp.where(m < 52, g[0], jnp.where(m < 124, g[1], g[2]))
            cost[pl.ds(row, 8), 128:256] = jnp.where(m < 68, g[2], g[3])

def aligned(x):
    return pl.multiple_of(x, 8)

def kernel_b(bases, costs, taps, start, occ_in, xh_in, yh_in, ch_in, cost, value, a1, a2, occ4, vb4, ct4, mt4, cl, vin, tmp_a, tmp_b, st, o4, ob, vst, occ, xh, yh, ch, pick, lhs, isem, osem, hsem):
    gx = lax.axis_index("gx"); gy = lax.axis_index("gy")
    r_lo = 20 - 256 * gy; r_hi = 20 + 256 * (lax.axis_size("gy") - gy)
    c_lo = 20 - 256 * gx; c_hi = 20 + 256 * (lax.axis_size("gx") - gx)
    halo_loads = [pltpu.make_async_copy(x, y, hsem.at[n]) for n, (x, y) in enumerate(((occ_in, occ), (xh_in, xh), (yh_in, yh), (ch_in, ch)))]
    for c in halo_loads:
        c.start()
    value_loads = [pltpu.make_async_copy(start.at[4 * n:4 * n + 4], vin.at[4 * n:4 * n + 4], isem.at[n]) for n in range(4)]
    for c in value_loads:
        c.start()
    for c in halo_loads:
        c.wait()
    occupied_tiles(occ, xh, yh, ch, occ4, (r_lo, r_hi, c_lo, c_hi))
    blur(taps, occ4, vb4, ct4, mt4, cost, (r_lo, r_hi, c_lo, c_hi))
    for s in range(LS):
        x = jnp.concatenate([mt4[q, pl.ds(s + K, NL, stride=LS), :] for q in range(NQ)], axis=0)
        cl[s] = jnp.transpose(x)[:XE]
    end = HV + 256 - 3 * XS
    b16 = jnp.bfloat16
    for j in range(2):
        src = lax.broadcasted_iota(i32, (256, 512), 0)
        dst = lax.broadcasted_iota(i32, (256, 512), 1)
        pick[256 * j:256 * j + 256, :] = jnp.where(src == (dst // 128) * XS + lax.rem(dst, 128) - HV, 1.0, 0.0).astype(b16)
    def build(tmp, t):
        hp = lax.rem(t, 8)
        sh = 16 * (t // 8)
        tile = hp // PER
        g = hp - PER * tile
        back = lax.rem(128 - HV * g, 128)
        fore = lax.rem(128 + end - HV * g, 128)
        def word(w):
            return (lax.shift_right_logical(w, jnp.full_like(w, sh)) & 0xFFFF).astype(f32) * (1.0 / CODE)
        def parts(row, v):
            n = v.shape[0]
            hi = v.astype(b16)
            lhs[row:row + n, 0:256] = hi
            lhs[row:row + n, 256:512] = (v - hi.astype(f32)).astype(b16)
        def put(rows, row, v, lh, rh):
            m = lane(rows)
            v[0] = jnp.where(m < HV, lh, v[0])
            v[3] = jnp.where(m < end, v[3], rh)
            for q in range(NQ):
                c = mt4[q, row:row + rows, :]
                tmp[q, row:row + rows, :] = jnp.where(c > 1e8, WALL, v[q] + c)
        k = t // PER
        gk = t - PER * k
        backk = lax.rem(128 - HV * gk, 128)
        forek = lax.rem(128 + end - HV * gk, 128)
        parts(0, vin[t])
        parts(256, jnp.concatenate([jnp.concatenate([word(yh[v, j, pl.ds(hp * 24 + c, 8), :]) for j in range(2)], axis=1)
            for v in range(2) for c in STEPS_V], axis=0))
        o = jnp.dot(lhs[...], pick[...], preferred_element_type=f32)
        o = [o[:, 128 * q:128 * q + 128] for q in range(NQ)]
        for i in range(2):
            wl = pltpu.roll(xh[0, k, i * 64:i * 64 + 64, :], backk, 1)
            wr = pltpu.roll(xh[1, k, i * 64:i * 64 + 64, :], forek, 1)
            for high in range(2):
                r = i * 64 + 128 * high
                put(64, r + HV, [e[r:r + 64] for e in o], value_of(wl, high), value_of(wr, high))
        n = 256
        for v in range(2):
            for c in STEPS_V:
                lh = word(pltpu.roll(ch[2 * v, tile, c:c + 8, :], back, 1))
                rh = word(pltpu.roll(ch[2 * v + 1, tile, c:c + 8, :], fore, 1))
                put(8, v * (HV + N) + c, [e[n:n + 8] for e in o], lh, rh)
                n += 8
    for c in value_loads:
        c.wait()
    build(tmp_a, 0)
    ri = lax.broadcasted_iota(i32, (XE, 256), 0)
    ci = lax.broadcasted_iota(i32, (XE, 256), 1)
    eye = jnp.where((ri == ci) | (ri + 128 == ci), 1.0, 0.0).astype(b16)
    def turn(tmp, t):
        for s in range(SE):
            x = jnp.concatenate([tmp[q, pl.ds(s, NL, stride=LS), :] for q in range(NQ)], axis=0)
            if s % MX == MX - 1:
                hi = x.astype(b16)
                lo = (x - hi.astype(f32)).astype(b16)
                y = lax.dot_general(eye, jnp.concatenate([hi, lo], axis=1), (((1,), (1,)), ((), ())), preferred_element_type=f32)
            else:
                y = jnp.transpose(x)[:XE]
            a1[pl.ds(aligned((t * SE + s) * XE), XE), :] = y
    @pl.loop(0, H // 2)
    def _(i):
        t = 2 * i
        build(tmp_b, t + 1)
        turn(tmp_a, t)
        build(tmp_a, jnp.minimum(t + 2, H - 1))
        turn(tmp_b, t + 1)
    def lowest(a, h, s0):
        acc = [None] * 3
        for p in range(P_SIZE):
            base = bases[h * P_SIZE + p] + s0 * XE
            c = costs[h * P_SIZE + p]
            for u in range(3):
                v = a[pl.ds(base + u * XE, XS), :] + c
                acc[u] = v if acc[u] is None else jnp.minimum(acc[u], v)
        return acc
    def halo(h):
        h = jnp.maximum(h, 0)
        slot = lax.rem(h, 2)
        for s in range(LS):
            rows = [st[slot, s, pl.ds(r, 8), :] for r in (XS, XS + 2, K, K + 2)]
            for r, v, n in zip((0, 2, XS + K, XS + K + 2), rows, (NL, NL, 128 - NL, 128 - NL)):
                st[slot, s, pl.ds(r, 8), :] = pltpu.roll(v, n, 1)
        for s in range(LS):
            full = st[slot, s]
            def put(k, v):
                a2[pl.ds(aligned(h * (SE * XE) + k * XE), XE), :] = v
            put(s + K, full)
            put(s + K - LS, pltpu.roll(full, 1, 1))
            put(s + K + LS, pltpu.roll(full, 127, 1))
            if s == LS - 1:
                put(0, pltpu.roll(full, 2, 1))
            if s == 0:
                put(SE - 1, pltpu.roll(full, 126, 1))
    @pl.loop(0, H)
    def _(h):
        halo(h - 1)
        slot = lax.rem(h, 2)
        for s0 in range(0, LS, 3):
            acc = lowest(a1, h, s0)
            for u in range(3):
                c = cl[s0 + u, K:K + XS, :]
                st[slot, s0 + u, K:K + XS, :] = jnp.where(c > 1e8, WALL, acc[u] + c)
    halo(H - 1)
    def vstore(h):
        return pltpu.make_async_copy(vst.at[lax.rem(h, 2)], value.at[h], osem.at[lax.rem(h, 2)])
    m = lane()
    def back(h):
        slot = lax.rem(h, 2)
        for s in range(LS):
            x = jnp.transpose(ob[slot, s])
            for q in range(NQ):
                o4[slot, q, pl.ds(s, NL, stride=LS), :] = x[q * NL:(q + 1) * NL]
    def assemble(h):
        slot = lax.rem(h, 2)
        for i in range(32):
            v = [o4[slot, q, pl.ds(i * 8 + K, 8), :] for q in range(NQ)]
            v = [pltpu.roll(w, n, 1) for w, n in zip(v, (118, 62, 6, 78))]
            vst[slot, i * 8:i * 8 + 8, 0:128] = jnp.where(m < 62, v[0], v[1])
            vst[slot, i * 8:i * 8 + 8, 128:256] = jnp.where(m < 6, v[1], jnp.where(m < 78, v[2], v[3]))
    @pl.loop(0, H)
    def _(h):
        @pl.when(h >= 4)
        def _():
            vstore(h - 4).wait()
        assemble(lax.rem(h, 2))
        back(lax.rem(h + 1, 2))
        slot = lax.rem(h, 2)
        for s0 in range(0, LS, 3):
            acc = lowest(a2, h, s0)
            for u in range(3):
                ob[slot, s0 + u, 0:XS, :] = acc[u]
        @pl.when(h >= 2)
        def _():
            vstore(h - 2).start()
    for h in (H, H + 1):
        vstore(h - 4).wait()
        assemble(h - 2)
        vstore(h - 2).start()
        if h == H:
            back(h - 1)
    vstore(H - 2).wait()
    vstore(H - 1).wait()

def call_b(bases, costs, blur_taps, start, occ, xh, yh, ch):
    S = pltpu.SMEM; V = pltpu.VMEM
    sp = lambda m: pl.BlockSpec(memory_space=m)
    return pl.pallas_call(
        kernel_b,
        out_shape=(jax.ShapeDtypeStruct((N, N), f32), jax.ShapeDtypeStruct((H, N, N), f32)),
        in_specs=[sp(S), sp(S), sp(S)] + [sp(pl.ANY)] * 5,
        out_specs=(sp(V), sp(pl.ANY)),
        scratch_shapes=[V((H * SE * XE, 128), f32), V((H * SE * XE, 128), f32), V((NQ, 328, 128), f32), V((NQ, 312, 128), f32),
            V((NQ, 312, 128), f32), V((NQ, 312, 128), f32), V((LS, XE, 128), f32),
            V((H, N, N), f32), V((NQ, 312, 128), f32), V((NQ, 312, 128), f32), V((2, LS, XE, 128), f32), V((2, NQ, NL * LS, 128), f32), V((2, LS, 128, 128), f32),
            V((2, N, N), f32), V((N, N), i32), V((2, 3, 128, 128), i32), V((2, 2, 208, 128), i32), V((4, 2, 24, 128), i32), V((512, 512), jnp.bfloat16), V((304, 512), jnp.bfloat16),
            pltpu.SemaphoreType.DMA((4,)), pltpu.SemaphoreType.DMA((2,)), pltpu.SemaphoreType.DMA((4,))],
        compiler_params=pltpu.CompilerParams(vmem_limit_bytes=63 * 2**20),
    )(bases, costs, blur_taps, start, occ, xh, yh, ch)

def shards(occupancy, blur_taps, offsets, step_costs, value_start):
    moves = (offsets[:, :, 0] + K) * XE + offsets[:, :, 1] + K
    xh, yh, ch, bases, costs = halos(moves, step_costs, value_start, occupancy)
    return call_b(bases, costs, blur_taps, value_start, occupancy, xh, yh, ch)


def solution(mesh):
    placed = (P("gy", "gx"), P(), P(), P(), P(None, "gy", "gx"))
    return jax.shard_map(shards, mesh=mesh, in_specs=placed, out_specs=(P("gy", "gx"), P(None, "gy", "gx")), check_vma=False)
```
